32 devices in a mesh: hel: 4 (over y, x), ang: 8 (over z, core).
Axes of the slice: x: 2, y: 2, z: 4, core: 2. Of those that a mesh axis runs over, the one named last changes fastest.
Arguments:
- wavepacket: float32 [64, 128, 32, 256], P('hel', 'ang'), may hold values from -6 to 6
- potential: float32 [128, 32, 256], P('ang'), may hold values from -0.4 to 0.4
- kinetic: float32 [256, 256], replicated, may hold values from -0.25 to 0.25
- ang_basis: float32 [64, 128, 128], P('hel'), may hold values from -1 to 1, as said below
- rot_energy: float32 [128], replicated, may hold values from -0.9 to -0.1
- radial_weight: float32 [256], replicated, may hold values from 0.2 to 1
- distance_weight: float32 [32], replicated, may hold values from 0.25 to 1
- truncation: int32 [64], P('hel'), may hold values from 32 to 128, as said below
- coupling: float32 [64], replicated, may hold values from 0.1 to 0.4
Outputs:
- evolved: float32 [64, 128, 32, 256], P('hel', 'ang')
The draws below stay inside these ranges and needn't reach their ends.
Inputs may be any that keep to these rules, and one draw needn't show every extreme that they name: Each ang_basis[k] is an orthogonal matrix. `truncation`: some helicity retains all 128 functions and some retains a quarter of them.
All inputs are finite; a program needn't handle non-finite values.
Results may differ from the reference program's by a relative error of at most 0.00011.
Values sent between devices are 32-bit elements; how exact they have to be, the bound alone decides.
No kernel may reach another device: no remote copies, remote signals or barrier semaphores. Data moves between devices by JAX's collectives and lax.ppermute only.
A program may use at most 128 MiB of HBM per device.

```python
import math
import jax
import jax.numpy as jnp
from jax import lax

K = 64
J = 128
NR = 256
RC = 32
OUTER = 3
INNER = 1


def draw_kinetic(key, part):
    normal_part = jax.random.truncated_normal(key, -4.0, 4.0, (NR, NR), jnp.float32)
    factor = 0.45 / math.sqrt(2.0 * NR)
    return (factor * 0.5 * (normal_part + normal_part.T)).astype(jnp.float32)


def draw_ang_basis(key, part):
    normal_part = jax.random.normal(key, (K, J, J), jnp.float32)
    orthogonal, upper = jnp.linalg.qr(normal_part)
    return orthogonal.astype(jnp.float32)


def draw_truncation(key, part):
    values = jax.random.randint(jax.random.fold_in(key, 11), (K,), J // 4, J + 1, jnp.int32)
    order = jax.random.permutation(jax.random.fold_in(key, 12), K)
    values = values.at[order[0]].set(J)
    values = values.at[order[1]].set(J // 4)
    return values.astype(jnp.int32)


def block_scale(rng, shape, cuts, least, largest):
    factor_of = 1.0
    for axis_at, shards_of in cuts:
        draws = jax.random.uniform(jax.random.fold_in(jax.random.fold_in(rng, 6), axis_at), (shards_of,), jnp.float32, least / len(cuts), largest / len(cuts))
        factor_of = factor_of * jnp.repeat(jnp.exp(draws), shape[axis_at] // shards_of).reshape((-1,) + (1,) * (len(shape) - 1 - axis_at))
    return factor_of


def gaussian(own_key, shape, deviation, most, pieces=(), held_as=jnp.bfloat16):
    values = deviation * jax.random.normal(own_key, shape, jnp.float32)
    if pieces:
        values = values * block_scale(own_key, shape, pieces, -0.22, 0.18)
    return jnp.clip(values, -most, most).astype(held_as)


def setup_inputs(seed: int = 0) -> dict:
    splits = jax.random.split(jax.random.key(seed), 10)
    return {
        "wavepacket": gaussian(splits[0], (K, J, RC, NR), 1.0, 6.0, ((0, 4), (1, 8)), jnp.float32),
        "potential": jnp.clip(jax.random.uniform(splits[1], (J, RC, NR), jnp.float32, -0.4, 0.4) * block_scale(splits[1], (J, RC, NR), ((0, 8),), -0.4, 0.0), -0.4, 0.4),
        "kinetic": draw_kinetic(jax.random.fold_in(splits[9], 71), 0),
        "ang_basis": draw_ang_basis(jax.random.fold_in(splits[9], 71), 0),
        "rot_energy": jnp.clip(jax.random.uniform(splits[4], (J,), jnp.float32, -0.9, -0.1), -0.9, -0.1),
        "radial_weight": jnp.clip(jnp.exp(jax.random.uniform(splits[5], (NR,), jnp.float32, math.log(0.2), math.log(1.0))), 0.2, 1.0),
        "distance_weight": jnp.clip(jnp.exp(jax.random.uniform(splits[6], (RC,), jnp.float32, math.log(0.25), math.log(1.0))), 0.25, 1.0),
        "truncation": draw_truncation(jax.random.fold_in(splits[9], 71), 0),
        "coupling": jnp.clip(jax.random.uniform(splits[8], (K,), jnp.float32, 0.1, 0.4), 0.1, 0.4),
    }


def hamiltonian(field, potential, kinetic):
    return jnp.dot(field.astype(jnp.float32), kinetic.astype(jnp.float32), precision=lax.Precision.HIGHEST, preferred_element_type=jnp.float32) + potential * field

def chebyshev(field, potential, kinetic):
    first = hamiltonian(field, potential, kinetic)
    second = 2.0 * hamiltonian(first, potential, kinetic) - field
    return 0.6 * field + 0.3 * first - 0.1 * second

def angular(field, basis, scale):
    coeffs = jnp.einsum('ji,irs->jrs', basis, field, precision=lax.Precision.HIGHEST)
    return field + jnp.einsum('ji,jrs->irs', basis, coeffs * scale[:, None, :], precision=lax.Precision.HIGHEST)

def coriolis(field, coupling, distance_weight):
    zero_slab = jnp.zeros_like(field[:1])
    upper_side = jnp.concatenate([field[1:], zero_slab], axis=0)
    lower_side = jnp.concatenate([zero_slab, field[:-1]], axis=0)
    before = jnp.concatenate([jnp.zeros((1,), jnp.float32), coupling[:-1]])
    return field + distance_weight[None, None, :, None] * (coupling[:, None, None, None] * upper_side + before[:, None, None, None] * lower_side)

def reference(wavepacket, potential, kinetic, ang_basis, rot_energy, radial_weight, distance_weight, truncation, coupling):
    orders = jnp.arange(J, dtype=jnp.int32)
    mask = (orders[None, :] < truncation[:, None]).astype(jnp.float32)
    scale_all = mask[:, :, None] * rot_energy[None, :, None] * radial_weight[None, None, :]

    def per_helicity(item):
        field, basis, scale = item
        for inner_turn in range(INNER):
            field = chebyshev(field, potential, kinetic)
            field = angular(field, basis, scale)
        return field
    field = wavepacket
    for outer_turn in range(OUTER):
        field = coriolis(field, coupling, distance_weight)
        field = lax.map(per_helicity, (field, ang_basis, scale_all))
    return field
```

```python
import jax
import jax.numpy as jnp
from jax import lax
from jax.experimental import pallas as pl
from jax.experimental.pallas import tpu as pltpu
from jax.sharding import PartitionSpec as P


OUTER = 3
PAIR = 2
LANES = 128


def partner(array, axis, bits):
    size = lax.axis_size(axis)
    return lax.ppermute(array, axis, [(i, i ^ bits) for i in range(size)])


def pack(wave, potential, chunk, places):
    count, angles, _, width = wave.shape
    size = lax.axis_size("ang")

    def kernel(place_ref, wave_ref, pot_ref, *outs):
        for d in range(size):
            start = place_ref[d]
            for k in range(count):
                rows = wave_ref.at[k].reshape(angles * size, LANES)
                outs[d][k] = rows[pl.ds(start, angles, stride=size), :]
            rows = pot_ref.reshape(angles * size, LANES)
            outs[d][count] = rows[pl.ds(start, angles, stride=size), :]

    return pl.pallas_call(
        kernel,
        name="pack",
        grid=(width // LANES,),
        in_specs=[
            pl.BlockSpec(memory_space=pltpu.SMEM),
            pl.BlockSpec((count, angles, size, LANES), lambda g: (0, 0, chunk, g)),
            pl.BlockSpec((angles, size, LANES), lambda g: (0, chunk, g)),
        ],
        out_specs=[pl.BlockSpec((count + 1, angles, LANES), lambda g: (0, 0, g))] * size,
        out_shape=[jax.ShapeDtypeStruct((count + 1, angles, width), jnp.float32)] * size,
    )(places, wave, potential)


def unpack(pieces, whole, shape, chunk, places):
    count, angles, _, width = shape
    size = len(pieces)

    def kernel(place_ref, *refs):
        ins, out = refs[:size], refs[-1]
        for d in range(size):
            start = place_ref[d]
            for k in range(count):
                rows = out.at[k].reshape(angles * size, LANES)
                rows[pl.ds(start, angles, stride=size), :] = ins[d][k]

    args = [places, *pieces]
    specs = [pl.BlockSpec(memory_space=pltpu.SMEM)] + [
        pl.BlockSpec((count, angles, LANES), lambda g: (0, 0, g))
    ] * size
    aliases = {}
    if whole is not None:
        aliases = {len(args): 0}
        args.append(whole)
        specs.append(pl.BlockSpec(memory_space=pl.ANY))
    return pl.pallas_call(
        kernel,
        name="unpack",
        grid=(width // LANES,),
        in_specs=specs,
        out_specs=pl.BlockSpec((count, angles, size, LANES), lambda g: (0, 0, chunk, g)),
        out_shape=jax.ShapeDtypeStruct(shape, jnp.float32),
        input_output_aliases=aliases,
    )(*args)


def halves(values):
    high = values.astype(jnp.bfloat16)
    return high, (values - high.astype(jnp.float32)).astype(jnp.bfloat16)


def window(pieces, below, above, mats, mats_below, mats_above, kinetic, radial, weights, places):
    size = len(pieces)
    count, angles, width = pieces[0].shape
    count -= 1
    full = size * angles
    total = count + 2 * OUTER

    def kernel(*refs):
        place_ref, weight_ref, kin_ref, rad_ref = refs[:4]
        ins = refs[4 : 4 + size]
        below_ref, above_ref, mat_ref, mat_below_ref, mat_above_ref = refs[4 + size : 9 + size]
        outs = refs[9 + size : 9 + 2 * size]
        one, two, mat, pot, kin, sems = refs[9 + 2 * size :]
        copies = []

        def fetch(source, target):
            copy = pltpu.make_async_copy(source, target, sems.at[len(copies)])
            copy.start()
            copies.append(copy)

        def spot(d):
            return pl.ds(pl.multiple_of(place_ref[d] * angles, angles), angles)

        for d in range(size):
            fetch(ins[d].at[pl.ds(0, count)], one.at[pl.ds(OUTER, count), spot(d), :])
            fetch(ins[d].at[count], pot.at[spot(d), :])
            fetch(below_ref.at[d], one.at[pl.ds(0, OUTER), spot(d), :])
            fetch(above_ref.at[d], one.at[pl.ds(OUTER + count, OUTER), spot(d), :])
        fetch(mat_below_ref, mat.at[pl.ds(0, OUTER)])
        fetch(mat_ref, mat.at[pl.ds(OUTER, count)])
        fetch(mat_above_ref, mat.at[pl.ds(OUTER + count, OUTER)])
        kin_high, kin_low = halves(kin_ref[...])
        kin[0], kin[1] = kin_high, kin_low
        for copy in copies:
            copy.wait()

        def times_kinetic(field):
            high, low = halves(field)
            dot = lambda a, b: jnp.dot(a, b, preferred_element_type=jnp.float32)
            return dot(high, kin[0]) + dot(low, kin[0]) + dot(high, kin[1])

        def step(source, target, turn):
            first = turn + 1
            amount = total - 2 * first
            potential = pot[...]
            spread = jnp.concatenate([potential] * PAIR, axis=0)

            def body(index, carry):
                m = first + index * PAIR
                fields = []
                for p in range(PAIR):
                    at = m + p - turn
                    fields.append(
                        source[at] + weight_ref[m + p + 1] * source[at + 1] + weight_ref[m + p] * source[at - 1]
                    )
                field = jnp.concatenate(fields, axis=0)
                once = times_kinetic(field) + spread * field
                mixed = 0.3 * field - 0.2 * once
                passed = 0.7 * field + times_kinetic(mixed) + spread * mixed
                for p in range(PAIR):
                    part = passed[p * full : (p + 1) * full]
                    high, low = halves(part)
                    mat_high, mat_low = halves(mat[m + p])
                    left = jnp.concatenate(
                        [
                            jnp.concatenate([mat_high, mat_high], axis=1),
                            jnp.concatenate([mat_low, mat_low], axis=1),
                        ],
                        axis=0,
                    )
                    both = jnp.dot(
                        left, jnp.concatenate([high, low], axis=0), preferred_element_type=jnp.float32
                    )
                    target[m + p - first] = part + rad_ref[...] * (both[:full] + both[full:])
                return carry

            lax.fori_loop(0, amount // PAIR, body, 0)

        buffers = [one, two]
        for turn in range(OUTER):
            step(buffers[turn % 2], buffers[(turn + 1) % 2], turn)
        result = buffers[OUTER % 2]
        stores = []
        for d in range(size):
            copy = pltpu.make_async_copy(result.at[pl.ds(0, count), spot(d), :], outs[d], sems.at[d])
            copy.start()
            stores.append(copy)
        for copy in stores:
            copy.wait()

    anywhere = pl.BlockSpec(memory_space=pl.ANY)
    return pl.pallas_call(
        kernel,
        name="window",
        in_specs=[
            pl.BlockSpec(memory_space=pltpu.SMEM),
            pl.BlockSpec(memory_space=pltpu.SMEM),
            pl.BlockSpec(memory_space=pltpu.VMEM),
            pl.BlockSpec(memory_space=pltpu.VMEM),
        ]
        + [anywhere] * (size + 5),
        out_specs=[anywhere] * size,
        out_shape=[jax.ShapeDtypeStruct((count, angles, width), jnp.float32)] * size,
        scratch_shapes=[
            pltpu.VMEM((total, full, width), jnp.float32),
            pltpu.VMEM((total, full, width), jnp.float32),
            pltpu.VMEM((total, full, full), jnp.float32),
            pltpu.VMEM((full, width), jnp.float32),
            pltpu.VMEM((2, width, width), jnp.bfloat16),
            pltpu.SemaphoreType.DMA((4 * size + 3,)),
        ],
    )(places, weights, kinetic, radial, *pieces, below, above, mats, mats_below, mats_above)


def edges(pieces):
    size = len(pieces)
    count, angles, width = pieces[0].shape
    count -= 1

    def kernel(*refs):
        ins, lows, highs, sems = refs[:size], refs[size], refs[size + 1], refs[size + 2]
        copies = []
        for d in range(size):
            for side, (target, start) in enumerate(((lows, 0), (highs, count - OUTER))):
                copies.append(
                    pltpu.make_async_copy(
                        ins[d].at[pl.ds(start, OUTER)], target.at[d], sems.at[2 * d + side]
                    )
                )
                copies[-1].start()
        for copy in copies:
            copy.wait()

    anywhere = pl.BlockSpec(memory_space=pl.ANY)
    shape = jax.ShapeDtypeStruct((size, OUTER, angles, width), jnp.float32)
    return pl.pallas_call(
        kernel,
        name="edges",
        in_specs=[anywhere] * size,
        out_specs=[anywhere] * 2,
        out_shape=[shape] * 2,
        scratch_shapes=[pltpu.SemaphoreType.DMA((2 * size,))],
    )(*pieces)


def along_hel(array, step):
    size = lax.axis_size("hel")
    return lax.ppermute(array, "hel", [(i, i + step) for i in range(size) if 0 <= i + step < size])


def body(
    wavepacket,
    potential,
    kinetic,
    ang_basis,
    rot_energy,
    radial_weight,
    distance_weight,
    truncation,
    coupling,
):
    count, _, cells, _ = wavepacket.shape
    size = lax.axis_size("ang")
    me = lax.axis_index("ang")
    chunks = cells // size
    places = jnp.bitwise_xor(me, jnp.arange(size, dtype=jnp.int32))

    received = []
    for c in range(chunks):
        sent = pack(wavepacket, potential, c, places)
        received.append([sent[d] if d == 0 else partner(sent[d], "ang", d) for d in range(size)])

    orders = jnp.arange(ang_basis.shape[1], dtype=jnp.int32)
    mask = (orders[None, :] < truncation[:, None]).astype(jnp.float32)
    factor = mask * rot_energy[None, :]
    mats = jnp.einsum(
        "kji,kjm->kim", ang_basis * factor[:, :, None], ang_basis, precision=lax.Precision.HIGHEST
    )
    mats_below = along_hel(mats[-OUTER:], 1)
    mats_above = along_hel(mats[:OUTER], -1)

    first = lax.axis_index("hel") * count
    ends = jnp.concatenate([jnp.zeros((OUTER + 1,)), coupling[:-1], jnp.zeros((OUTER + 1,))])
    near = lax.dynamic_slice_in_dim(ends, first, count + 2 * OUTER + 1)
    out = None
    for c in range(chunks):
        pieces = received[c]
        if c:
            pieces = lax.optimization_barrier((*pieces, done[0]))[:-1]
        lows, highs = edges(pieces)
        below = along_hel(highs, 1)
        above = along_hel(lows, -1)
        weights = near * lax.dynamic_index_in_dim(distance_weight, c * size + me, keepdims=False)
        done = window(
            pieces, below, above, mats, mats_below, mats_above, kinetic, radial_weight[None], weights, places
        )
        back = [done[d] if d == 0 else partner(done[d], "ang", d) for d in range(size)]
        out = unpack(back, out, wavepacket.shape, c, places)
    return out


def solution(mesh):
    placed = (
        P("hel", "ang", None, None),
        P("ang", None, None),
        P(),
        P("hel", None, None),
        P(),
        P(),
        P(),
        P("hel"),
        P(),
    )
    whole = P("hel", "ang", None, None)
    return jax.shard_map(body, mesh=mesh, in_specs=placed, out_specs=whole, check_vma=False)
```

```python
import math

import jax
import jax.numpy as jnp
from jax import lax
from jax.experimental import pallas as pl
from jax.experimental.pallas import tpu as pltpu
from jax.sharding import PartitionSpec as P


OUTER = 3
PAIR = 2
LANES = 128


def partner(array, axis, bits):
    size = lax.axis_size(axis)
    return lax.ppermute(array, axis, [(i, i ^ bits) for i in range(size)])


def swap(arrays, axis, ranks):
    swapped = {d: partner(arrays[d], axis, d) for d in ranks}
    return [swapped.get(d, arrays[d]) for d in range(len(arrays))]


def spread_potential(potential, chunks, places):
    size, groups = lax.axis_size("ang"), lax.axis_size("hel")
    if chunks != groups:
        packed = pack(potential, tuple(range(chunks)), places)
        pieces = swap(packed, "ang", range(1, size))
        return [jnp.stack([piece[c] for piece in pieces]) for c in range(chunks)]
    group = lax.axis_index("hel")
    own = lax.dynamic_slice_in_dim(potential, group * size, size, axis=1)
    packed = pack(own, (0,), places)
    pieces = swap(packed, "ang", range(1, size))
    mine = jnp.concatenate(pieces)
    known = jnp.stack(swap([mine] * groups, "hel", range(1, groups)))
    return [lax.dynamic_index_in_dim(known, jnp.bitwise_xor(group, c), keepdims=False) for c in range(chunks)]


def pack(array, chunks, places):
    *_, angles, cells, width = array.shape
    lead = array.shape[:-3]
    count = math.prod(lead)
    size = lax.axis_size("ang")

    def kernel(place_ref, *refs):
        ins, outs = refs[: len(chunks)], refs[len(chunks) :]
        for d in range(size):
            start = place_ref[d]
            for c, block in enumerate(ins):
                for k in range(count):
                    view = block.at[k] if lead else block
                    rows = view.reshape(angles * size, LANES)
                    outs[d][c * count + k] = rows[pl.ds(start, angles, stride=size), :]

    def spec(chunk):
        shape = (*lead, angles, size, LANES)
        return pl.BlockSpec(shape, lambda g: (*(0 for _ in lead), 0, chunk, g))

    packed = (len(chunks) * count, angles, width)
    return pl.pallas_call(
        kernel,
        name="pack",
        grid=(width // LANES,),
        in_specs=[pl.BlockSpec(memory_space=pltpu.SMEM)] + [spec(chunk) for chunk in chunks],
        out_specs=[pl.BlockSpec((packed[0], angles, LANES), lambda g: (0, 0, g))] * size,
        out_shape=[jax.ShapeDtypeStruct(packed, jnp.float32)] * size,
    )(places, *[array] * len(chunks))


def unpack(pieces, whole, shape, chunk, places):
    count, angles, _, width = shape
    size = len(pieces)

    def kernel(place_ref, *refs):
        ins, out = refs[:size], refs[-1]
        for d in range(size):
            start = place_ref[d]
            for k in range(count):
                rows = out.at[k].reshape(angles * size, LANES)
                rows[pl.ds(start, angles, stride=size), :] = ins[d][k]

    args = [places, *pieces]
    specs = [pl.BlockSpec(memory_space=pltpu.SMEM)] + [
        pl.BlockSpec((count, angles, LANES), lambda g: (0, 0, g))
    ] * size
    aliases = {}
    if whole is not None:
        aliases = {len(args): 0}
        args.append(whole)
        specs.append(pl.BlockSpec(memory_space=pl.ANY))
    return pl.pallas_call(
        kernel,
        name="unpack",
        grid=(width // LANES,),
        in_specs=specs,
        out_specs=pl.BlockSpec((count, angles, size, LANES), lambda g: (0, 0, chunk, g)),
        out_shape=jax.ShapeDtypeStruct(shape, jnp.float32),
        input_output_aliases=aliases,
    )(*args)


def halves(values):
    high = values.astype(jnp.bfloat16)
    return high, (values - high.astype(jnp.float32)).astype(jnp.bfloat16)


def window(pieces, potential, below, above, mats, mats_below, mats_above, kinetic, radial, weights, places):
    size = len(pieces)
    count, angles, width = pieces[0].shape
    full = size * angles
    total = count + 2 * OUTER

    def kernel(*refs):
        place_ref, weight_ref, kin_ref, rad_ref = refs[:4]
        ins = refs[4 : 4 + size]
        pot_ref, below_ref, above_ref, mat_ref, mat_below_ref, mat_above_ref = refs[4 + size : 10 + size]
        outs = refs[10 + size : 10 + 2 * size]
        one, two, mat, pot, kin, sems = refs[10 + 2 * size :]
        copies = []

        def fetch(source, target):
            copy = pltpu.make_async_copy(source, target, sems.at[len(copies)])
            copy.start()
            copies.append(copy)

        def spot(d):
            return pl.ds(pl.multiple_of(place_ref[d] * angles, angles), angles)

        for d in range(size):
            fetch(ins[d], one.at[pl.ds(OUTER, count), spot(d), :])
            fetch(pot_ref.at[d], pot.at[spot(d), :])
            fetch(below_ref.at[d], one.at[pl.ds(0, OUTER), spot(d), :])
            fetch(above_ref.at[d], one.at[pl.ds(OUTER + count, OUTER), spot(d), :])
        fetch(mat_below_ref, mat.at[pl.ds(0, OUTER)])
        fetch(mat_ref, mat.at[pl.ds(OUTER, count)])
        fetch(mat_above_ref, mat.at[pl.ds(OUTER + count, OUTER)])
        kin_high, kin_low = halves(kin_ref[...])
        kin[0], kin[1] = kin_high, kin_low
        for copy in copies:
            copy.wait()

        def times_kinetic(field):
            high, low = halves(field)
            dot = lambda a, b: jnp.dot(a, b, preferred_element_type=jnp.float32)
            return dot(high, kin[0]) + dot(low, kin[0]) + dot(high, kin[1])

        def step(source, target, turn):
            first = turn + 1
            amount = total - 2 * first
            potential = pot[...]
            spread = jnp.concatenate([potential] * PAIR, axis=0)

            def body(index, carry):
                m = first + index * PAIR
                fields = []
                for p in range(PAIR):
                    at = m + p - turn
                    fields.append(
                        source[at] + weight_ref[m + p + 1] * source[at + 1] + weight_ref[m + p] * source[at - 1]
                    )
                field = jnp.concatenate(fields, axis=0)
                once = times_kinetic(field) + spread * field
                mixed = 0.3 * field - 0.2 * once
                passed = 0.7 * field + times_kinetic(mixed) + spread * mixed
                for p in range(PAIR):
                    part = passed[p * full : (p + 1) * full]
                    high, low = halves(part)
                    mat_high, mat_low = halves(mat[m + p])
                    left = jnp.concatenate(
                        [
                            jnp.concatenate([mat_high, mat_high], axis=1),
                            jnp.concatenate([mat_low, mat_low], axis=1),
                        ],
                        axis=0,
                    )
                    both = jnp.dot(
                        left, jnp.concatenate([high, low], axis=0), preferred_element_type=jnp.float32
                    )
                    target[m + p - first] = part + rad_ref[...] * (both[:full] + both[full:])
                return carry

            lax.fori_loop(0, amount // PAIR, body, 0)

        buffers = [one, two]
        for turn in range(OUTER):
            step(buffers[turn % 2], buffers[(turn + 1) % 2], turn)
        result = buffers[OUTER % 2]
        stores = []
        for d in range(size):
            copy = pltpu.make_async_copy(result.at[pl.ds(0, count), spot(d), :], outs[d], sems.at[d])
            copy.start()
            stores.append(copy)
        for copy in stores:
            copy.wait()

    anywhere = pl.BlockSpec(memory_space=pl.ANY)
    return pl.pallas_call(
        kernel,
        name="window",
        in_specs=[
            pl.BlockSpec(memory_space=pltpu.SMEM),
            pl.BlockSpec(memory_space=pltpu.SMEM),
            pl.BlockSpec(memory_space=pltpu.VMEM),
            pl.BlockSpec(memory_space=pltpu.VMEM),
        ]
        + [anywhere] * (size + 6),
        out_specs=[anywhere] * size,
        out_shape=[jax.ShapeDtypeStruct((count, angles, width), jnp.float32)] * size,
        scratch_shapes=[
            pltpu.VMEM((total, full, width), jnp.float32),
            pltpu.VMEM((total, full, width), jnp.float32),
            pltpu.VMEM((total, full, full), jnp.float32),
            pltpu.VMEM((full, width), jnp.float32),
            pltpu.VMEM((2, width, width), jnp.bfloat16),
            pltpu.SemaphoreType.DMA((4 * size + 3,)),
        ],
    )(places, weights, kinetic, radial, *pieces, potential, below, above, mats, mats_below, mats_above)


def edges(pieces):
    size = len(pieces)
    count, angles, width = pieces[0].shape

    def kernel(*refs):
        ins, lows, highs, sems = refs[:size], refs[size], refs[size + 1], refs[size + 2]
        copies = []
        for d in range(size):
            for side, (target, start) in enumerate(((lows, 0), (highs, count - OUTER))):
                copies.append(
                    pltpu.make_async_copy(
                        ins[d].at[pl.ds(start, OUTER)], target.at[d], sems.at[2 * d + side]
                    )
                )
                copies[-1].start()
        for copy in copies:
            copy.wait()

    anywhere = pl.BlockSpec(memory_space=pl.ANY)
    shape = jax.ShapeDtypeStruct((size, OUTER, angles, width), jnp.float32)
    return pl.pallas_call(
        kernel,
        name="edges",
        in_specs=[anywhere] * size,
        out_specs=[pl.BlockSpec(memory_space=pltpu.VMEM)] * 2,
        out_shape=[shape] * 2,
        scratch_shapes=[pltpu.SemaphoreType.DMA((2 * size,))],
    )(*pieces)


def along_hel(array, step):
    size = lax.axis_size("hel")
    return lax.ppermute(array, "hel", [(i, i + step) for i in range(size) if 0 <= i + step < size])


def body(
    wavepacket,
    potential,
    kinetic,
    ang_basis,
    rot_energy,
    radial_weight,
    distance_weight,
    truncation,
    coupling,
):
    count, _, cells, _ = wavepacket.shape
    size = lax.axis_size("ang")
    me = lax.axis_index("ang")
    chunks = cells // size
    places = jnp.bitwise_xor(me, jnp.arange(size, dtype=jnp.int32))

    ranks = sorted(range(1, size), key=lambda d: -(d // 2))
    received = []
    for c in range(chunks):
        sent = pack(wavepacket, (c,), places)
        received.append(swap(sent, "ang", ranks))
        if c == 0:
            potentials = spread_potential(potential, chunks, places)

    orders = jnp.arange(ang_basis.shape[1], dtype=jnp.int32)
    mask = (orders[None, :] < truncation[:, None]).astype(jnp.float32)
    factor = mask * rot_energy[None, :]
    mats = jnp.einsum(
        "kji,kjm->kim", ang_basis * factor[:, :, None], ang_basis, precision=lax.Precision.HIGHEST
    )
    mats_below = along_hel(mats[-OUTER:], 1)
    mats_above = along_hel(mats[:OUTER], -1)

    first = lax.axis_index("hel") * count
    ends = jnp.concatenate([jnp.zeros((OUTER + 1,)), coupling[:-1], jnp.zeros((OUTER + 1,))])
    near = lax.dynamic_slice_in_dim(ends, first, count + 2 * OUTER + 1)
    halos = {}
    done = {}

    def exchange(c):
        pieces = received[c]
        if c >= 2:
            pieces = lax.optimization_barrier((*pieces, done[c - 2][0]))[:-1]
        lows, highs = edges(pieces)
        halos[c] = pieces, along_hel(highs, 1), along_hel(lows, -1), lows

    exchange(0)
    backs = []
    for c in range(chunks):
        weights = near * lax.dynamic_index_in_dim(distance_weight, c * size + me, keepdims=False)
        pieces, below, above, _ = halos[c]
        if c + 1 < chunks:
            exchange(c + 1)
            weights, _ = lax.optimization_barrier((weights, halos[c + 1][3]))
        done[c] = window(
            pieces,
            potentials[c],
            below,
            above,
            mats,
            mats_below,
            mats_above,
            kinetic,
            radial_weight[None],
            weights,
            places,
        )
        backs.append(swap(done[c], "ang", ranks))
    out = None
    for c in range(chunks):
        out = unpack(backs[c], out, wavepacket.shape, c, places)
    return out


def solution(mesh):
    placed = (
        P("hel", "ang", None, None),
        P("ang", None, None),
        P(),
        P("hel", None, None),
        P(),
        P(),
        P(),
        P("hel"),
        P(),
    )
    whole = P("hel", "ang", None, None)
    return jax.shard_map(body, mesh=mesh, in_specs=placed, out_specs=whole, check_vma=False)
```

```python
import math

import jax
import jax.numpy as jnp
from jax import lax
from jax.experimental import pallas as pl
from jax.experimental.pallas import tpu as pltpu
from jax.sharding import PartitionSpec as P


OUTER = 3
GROUP = 6
LANES = 128


def swap(arrays, axis, ranks):
    size = lax.axis_size(axis)
    swapped = {}
    for d in ranks:
        swapped[d] = lax.ppermute(arrays[d], axis, [(i, i ^ d) for i in range(size)])
    return [swapped.get(d, arrays[d]) for d in range(size)]


def place(d):
    return jnp.bitwise_xor(lax.axis_index("ang"), d)


def pack(wave, chunk, span, potential=None):
    _, angles, cells, width = wave.shape
    start, stop = span
    block = math.gcd(start, stop) if potential is None else stop - start
    size = lax.axis_size("ang")
    extra = 0 if potential is None else len(slabs_of(cells // size))

    def kernel(*refs):
        wave_ref, outs = refs[0], refs[-size:]
        slabs = slabs_of(cells // size) if extra else []
        for d in range(size):
            first = place(d)
            for k in range(block):
                rows = wave_ref.at[k].reshape(angles * size, LANES)
                outs[d][k] = rows[pl.ds(first, angles, stride=size), :]
            for s, slab in enumerate(slabs):
                rows = refs[1].reshape(angles * cells, LANES)
                outs[d][block + s] = rows[pl.ds(slab * size + first, angles, stride=cells), :]

    args = [wave]
    specs = [pl.BlockSpec((block, angles, size, LANES), lambda k, g: (start // block + k, 0, chunk, g))]
    if extra:
        args.append(potential)
        specs.append(pl.BlockSpec((angles, cells, LANES), lambda k, g: (0, 0, g)))
    packed = (stop - start + extra, angles, width)
    return pl.pallas_call(
        kernel,
        name="pack",
        grid=((stop - start) // block, width // LANES),
        in_specs=specs,
        out_specs=[pl.BlockSpec((block + extra, angles, LANES), lambda k, g: (k, 0, g))] * size,
        out_shape=[jax.ShapeDtypeStruct(packed, jnp.float32)] * size,
    )(*args)


def unpack(pieces, whole, shape, chunk, span):
    _, angles, _, width = shape
    start, stop = span
    block = math.gcd(start, stop)
    size = len(pieces)

    def kernel(*refs):
        ins, out = refs[:size], refs[-1]
        for d in range(size):
            first = place(d)
            for k in range(block):
                rows = out.at[k].reshape(angles * size, LANES)
                rows[pl.ds(first, angles, stride=size), :] = ins[d][k]

    args = [*pieces]
    specs = [pl.BlockSpec((block, angles, LANES), lambda k, g: (k, 0, g))] * size
    aliases = {}
    if whole is not None:
        aliases = {len(args): 0}
        args.append(whole)
        specs.append(pl.BlockSpec(memory_space=pl.ANY))
    return pl.pallas_call(
        kernel,
        name="unpack",
        grid=((stop - start) // block, width // LANES),
        in_specs=specs,
        out_specs=pl.BlockSpec(
            (block, angles, size, LANES), lambda k, g: (start // block + k, 0, chunk, g)
        ),
        out_shape=jax.ShapeDtypeStruct(shape, jnp.float32),
        input_output_aliases=aliases,
    )(*args)


def slabs_of(chunks):
    return [lax.axis_index("hel")] if chunks == lax.axis_size("hel") else list(range(chunks))


def gather(arrays, start, stop):
    size = len(arrays)
    shape = (size, stop - start, *arrays[0].shape[1:])

    def kernel(*refs):
        ins, out, sems = refs[:size], refs[size], refs[size + 1]
        copies = [
            pltpu.make_async_copy(ins[d].at[pl.ds(start, stop - start)], out.at[d], sems.at[d])
            for d in range(size)
        ]
        for copy in copies:
            copy.start()
        for copy in copies:
            copy.wait()

    return pl.pallas_call(
        kernel,
        name="gather",
        in_specs=[pl.BlockSpec(memory_space=pl.ANY)] * size,
        out_specs=pl.BlockSpec(memory_space=pltpu.VMEM),
        out_shape=jax.ShapeDtypeStruct(shape, jnp.float32),
        scratch_shapes=[pltpu.SemaphoreType.DMA((size,))],
    )(*arrays)


def spread_potential(mine, chunks):
    groups = lax.axis_size("hel")
    if chunks != groups:
        return [mine[:, c] for c in range(chunks)]
    known = jnp.stack(swap([mine[:, 0]] * groups, "hel", range(1, groups)))
    group = lax.axis_index("hel")
    return [lax.dynamic_index_in_dim(known, jnp.bitwise_xor(group, c), keepdims=False) for c in range(chunks)]


def overlaps(spans, start, stop):
    for s, (low, high) in enumerate(spans):
        first, last = max(low, start), min(high, stop)
        if first < last:
            yield s, first - low, first - start, last - first


def edges(segments, spans):
    size = len(segments[0])
    _, angles, width = segments[0][0].shape
    count = spans[-1][1]
    jobs = [
        (side, *part)
        for side, start in enumerate((0, count - OUTER))
        for part in overlaps(spans, start, start + OUTER)
    ]

    def kernel(*refs):
        ins, targets, sems = refs[: size * len(spans)], refs[-3:-1], refs[-1]
        copies = []
        for d in range(size):
            for side, s, source, target, amount in jobs:
                copies.append(
                    pltpu.make_async_copy(
                        ins[s * size + d].at[pl.ds(source, amount)],
                        targets[side].at[d, pl.ds(target, amount)],
                        sems.at[len(copies)],
                    )
                )
                copies[-1].start()
        for copy in copies:
            copy.wait()

    shape = jax.ShapeDtypeStruct((size, OUTER, angles, width), jnp.float32)
    return pl.pallas_call(
        kernel,
        name="edges",
        in_specs=[pl.BlockSpec(memory_space=pl.ANY)] * (size * len(spans)),
        out_specs=[pl.BlockSpec(memory_space=pltpu.VMEM)] * 2,
        out_shape=[shape] * 2,
        scratch_shapes=[pltpu.SemaphoreType.DMA((len(jobs) * size,))],
    )(*[piece for segment in segments for piece in segment])


def halves(values):
    high = values.astype(jnp.bfloat16)
    return high, (values - high.astype(jnp.float32)).astype(jnp.bfloat16)


def window(segments, spans, result_spans, potential, below, above, mats, mats_below, mats_above, kinetic, radial, weights):
    size = len(segments[0])
    _, angles, width = segments[0][0].shape
    count = spans[-1][1]
    full = size * angles
    total = count + 2 * OUTER
    n_in, n_out = size * len(spans), size * len(result_spans)

    def kernel(*refs):
        weight_ref, kin_ref, rad_ref = refs[:3]
        ins = refs[3 : 3 + n_in]
        pot_ref, below_ref, above_ref, mat_ref, mat_below_ref, mat_above_ref = refs[3 + n_in : 9 + n_in]
        outs = refs[9 + n_in : 9 + n_in + n_out]
        one, two, mat, pot, kin, sems = refs[9 + n_in + n_out :]
        copies = []

        def fetch(source, target):
            copy = pltpu.make_async_copy(source, target, sems.at[len(copies)])
            copy.start()
            copies.append(copy)

        def spot(d):
            return pl.ds(pl.multiple_of(place(d) * angles, angles), angles)

        for d in range(size):
            for s, (start, stop) in enumerate(spans):
                fetch(ins[s * size + d].at[pl.ds(0, stop - start)], one.at[pl.ds(OUTER + start, stop - start), spot(d), :])
            fetch(pot_ref.at[d], pot.at[spot(d), :])
            fetch(below_ref.at[d], one.at[pl.ds(0, OUTER), spot(d), :])
            fetch(above_ref.at[d], one.at[pl.ds(OUTER + count, OUTER), spot(d), :])
        fetch(mat_below_ref, mat.at[pl.ds(0, OUTER)])
        fetch(mat_ref, mat.at[pl.ds(OUTER, count)])
        fetch(mat_above_ref, mat.at[pl.ds(OUTER + count, OUTER)])
        kin_high, kin_low = halves(kin_ref[...])
        kin[0], kin[1] = kin_high, kin_low
        for copy in copies:
            copy.wait()

        def dot(a, b):
            return jnp.dot(a, b, preferred_element_type=jnp.float32)

        def times_kinetic(field):
            high, low = halves(field)
            return dot(high, kin[0]) + dot(low, kin[0]) + dot(high, kin[1])

        def step(source, target, turn):
            first = turn + 1
            amount = total - 2 * first

            def rows(m, group):
                fields = []
                for p in range(group):
                    at = m + p - turn
                    fields.append(
                        source[at] + weight_ref[m + p + 1] * source[at + 1] + weight_ref[m + p] * source[at - 1]
                    )
                field = jnp.concatenate(fields, axis=0)
                spread = jnp.concatenate([pot[...]] * group, axis=0)
                once = times_kinetic(field) + spread * field
                mixed = 0.3 * field - 0.2 * once
                passed = 0.7 * field + times_kinetic(mixed) + spread * mixed
                for p in range(group):
                    part = passed[p * full : (p + 1) * full]
                    high, low = halves(part)
                    rows = [jnp.concatenate([piece, piece], axis=1) for piece in halves(mat[m + p])]
                    both = dot(jnp.concatenate(rows, axis=0), jnp.concatenate([high, low], axis=0))
                    target[m + p - first] = part + rad_ref[...] * (both[:full] + both[full:])

            def body(index, carry):
                rows(first + index * GROUP, GROUP)
                return carry

            lax.fori_loop(0, amount // GROUP, body, 0)
            if amount % GROUP:
                rows(first + amount // GROUP * GROUP, amount % GROUP)

        buffers = [one, two]
        for turn in range(OUTER):
            step(buffers[turn % 2], buffers[(turn + 1) % 2], turn)
        result = buffers[OUTER % 2]
        stores = []
        for d in range(size):
            for s, (start, stop) in enumerate(result_spans):
                copy = pltpu.make_async_copy(
                    result.at[pl.ds(start, stop - start), spot(d), :], outs[s * size + d], sems.at[len(stores)]
                )
                copy.start()
                stores.append(copy)
        for copy in stores:
            copy.wait()

    anywhere = pl.BlockSpec(memory_space=pl.ANY)
    results = pl.pallas_call(
        kernel,
        name="window",
        in_specs=[
            pl.BlockSpec(memory_space=pltpu.SMEM),
            pl.BlockSpec(memory_space=pltpu.VMEM),
            pl.BlockSpec(memory_space=pltpu.VMEM),
        ]
        + [anywhere] * (n_in + 6),
        out_specs=[anywhere] * n_out,
        out_shape=[
            jax.ShapeDtypeStruct((stop - start, angles, width), jnp.float32)
            for start, stop in result_spans
            for _ in range(size)
        ],
        scratch_shapes=[
            pltpu.VMEM((total, full, width), jnp.float32),
            pltpu.VMEM((total, full, width), jnp.float32),
            pltpu.VMEM((total, full, full), jnp.float32),
            pltpu.VMEM((full, width), jnp.float32),
            pltpu.VMEM((2, width, width), jnp.bfloat16),
            pltpu.SemaphoreType.DMA((max(n_in, n_out) + 3 * size + 3,)),
        ],
    )(
        weights,
        kinetic,
        radial,
        *[piece for segment in segments for piece in segment],
        potential,
        below,
        above,
        mats,
        mats_below,
        mats_above,
    )
    return [results[s * size : (s + 1) * size] for s in range(len(result_spans))]


def along_hel(array, step):
    size = lax.axis_size("hel")
    return lax.ppermute(array, "hel", [(i, i + step) for i in range(size) if 0 <= i + step < size])


def body(
    wavepacket,
    potential,
    kinetic,
    ang_basis,
    rot_energy,
    radial_weight,
    distance_weight,
    truncation,
    coupling,
):
    count, _, cells, _ = wavepacket.shape
    size = lax.axis_size("ang")
    chunks = cells // size
    ranks = sorted(range(1, size), key=lambda d: -(d // 2))
    quarter = max(count // 4, 1)
    spans = [[(0, count)] for _ in range(chunks)]
    spans[0] = [(0, quarter), (quarter, count)]
    result_spans = [[(0, count)] for _ in range(chunks)]
    result_spans[-1] = [(0, count - quarter), (count - quarter, count)]

    received = []
    for c in range(chunks):
        segments = []
        for s, span in enumerate(spans[c]):
            sent = pack(wavepacket, c, span, potential if (c, s) == (0, 0) else None)
            segments.append(swap(sent, "ang", ranks))
        received.append(segments)
    slabs = len(slabs_of(chunks))
    potentials = spread_potential(gather(received[0][0], quarter, quarter + slabs), chunks)

    orders = jnp.arange(ang_basis.shape[1], dtype=jnp.int32)
    mask = (orders[None, :] < truncation[:, None]).astype(jnp.float32)
    factor = mask * rot_energy[None, :]
    mats = jnp.einsum(
        "kji,kjm->kim", ang_basis * factor[:, :, None], ang_basis, precision=lax.Precision.HIGHEST
    )
    mats_below = along_hel(mats[-OUTER:], 1)
    mats_above = along_hel(mats[:OUTER], -1)

    first = lax.axis_index("hel") * count
    ends = jnp.concatenate([jnp.zeros((OUTER + 1,)), coupling[:-1], jnp.zeros((OUTER + 1,))])
    near = lax.dynamic_slice_in_dim(ends, first, count + 2 * OUTER + 1)
    halos = {}
    done = {}

    def exchange(c):
        segments = received[c]
        if c >= 2:
            segments, _ = lax.optimization_barrier((segments, done[c - 2][0][0]))
        lows, highs = edges(segments, spans[c])
        halos[c] = segments, along_hel(highs, 1), along_hel(lows, -1), lows

    exchange(0)
    backs = []
    for c in range(chunks):
        weights = near * lax.dynamic_index_in_dim(
            distance_weight, c * size + lax.axis_index("ang"), keepdims=False
        )
        segments, below, above, _ = halos[c]
        if c + 1 < chunks:
            exchange(c + 1)
            weights, _ = lax.optimization_barrier((weights, halos[c + 1][3]))
        done[c] = window(
            segments,
            spans[c],
            result_spans[c],
            potentials[c],
            below,
            above,
            mats,
            mats_below,
            mats_above,
            kinetic,
            radial_weight[None],
            weights,
        )
        for s, segment in enumerate(done[c]):
            backs.append((swap(segment, "ang", ranks), c, result_spans[c][s]))
    out = None
    for back, c, span in backs:
        out = unpack(back, out, wavepacket.shape, c, span)
    return out


def solution(mesh):
    placed = (
        P("hel", "ang", None, None),
        P("ang", None, None),
        P(),
        P("hel", None, None),
        P(),
        P(),
        P(),
        P("hel"),
        P(),
    )
    whole = P("hel", "ang", None, None)
    return jax.shard_map(body, mesh=mesh, in_specs=placed, out_specs=whole, check_vma=False)
```

```python
import math

import jax
import jax.numpy as jnp
from jax import lax
from jax.experimental import pallas as pl
from jax.experimental.pallas import tpu as pltpu
from jax.sharding import PartitionSpec as P


OUTER = 3
GROUP = 4
GRANT = 24 << 20
LANES = 128


def swap(arrays, axis, ranks):
    size = lax.axis_size(axis)
    swapped = {}
    for d in ranks:
        swapped[d] = lax.ppermute(arrays[d], axis, [(i, i ^ d) for i in range(size)])
    return [swapped.get(d, arrays[d]) for d in range(size)]


def place(d):
    return jnp.bitwise_xor(lax.axis_index("ang"), d)


def pack(wave, chunk, span, potential=None):
    _, angles, cells, width = wave.shape
    start, stop = span
    block = math.gcd(start, stop, max(wave.shape[0] // 4, 1))
    many = 1 if potential is None else (stop - start) // block
    size = lax.axis_size("ang")
    extra = 0 if potential is None else len(slabs_of(cells // size))

    lanes = width // LANES

    def kernel(*refs):
        waves, outs = refs[: many * lanes], refs[-size:]
        slabs = slabs_of(cells // size) if extra else []
        for d in range(size):
            first = place(d)
            for g in range(lanes):
                columns = slice(g * LANES, (g + 1) * LANES)
                for k in range(many * block):
                    rows = waves[k // block * lanes + g].at[k % block].reshape(angles * size, LANES)
                    outs[d][k, :, columns] = rows[pl.ds(first, angles, stride=size), :]
                for s, slab in enumerate(slabs):
                    rows = refs[many * lanes + g].reshape(angles * cells, LANES)
                    outs[d][many * block + s, :, columns] = rows[pl.ds(slab * size + first, angles, stride=cells), :]

    def wave_spec(j, g):
        return pl.BlockSpec(
            (block, angles, size, LANES), lambda k: (start // block + k * many + j, 0, chunk, g)
        )

    def potential_spec(g):
        return pl.BlockSpec((angles, cells, LANES), lambda k: (0, 0, g))

    args = [pltpu.with_memory_space_constraint(wave, pltpu.HBM)] * (many * lanes)
    specs = [wave_spec(j, g) for j in range(many) for g in range(lanes)]
    if extra:
        args += [pltpu.with_memory_space_constraint(potential, pltpu.HBM)] * lanes
        specs += [potential_spec(g) for g in range(lanes)]
    packed = (stop - start + extra, angles, width)
    return pl.pallas_call(
        kernel,
        name="pack",
        compiler_params=pltpu.CompilerParams(vmem_limit_bytes=GRANT),
        grid=((stop - start) // (many * block),),
        in_specs=specs,
        out_specs=[pl.BlockSpec((many * block + extra, angles, width), lambda k: (k, 0, 0))] * size,
        out_shape=[jax.ShapeDtypeStruct(packed, jnp.float32)] * size,
    )(*args)


def unpack(pieces, whole, shape, chunk, span):
    _, angles, _, width = shape
    start, stop = span
    amount = stop - start
    size = len(pieces)
    lanes = width // LANES

    def kernel(*refs):
        ins, out, parts, sems = refs[:size], refs[-3], refs[-2], refs[-1]
        copies = []
        for g in range(lanes):
            columns = slice(g * LANES, (g + 1) * LANES)
            for d in range(size):
                first = place(d)
                for k in range(amount):
                    rows = parts.at[g, k].reshape(angles * size, LANES)
                    rows[pl.ds(first, angles, stride=size), :] = ins[d][k, :, columns]
            copies.append(
                pltpu.make_async_copy(
                    parts.at[g],
                    out.at[pl.ds(start, amount), :, pl.ds(chunk * size, size), pl.ds(g * LANES, LANES)],
                    sems.at[g],
                )
            )
            copies[-1].start()
        for copy in copies:
            copy.wait()

    args = [*pieces]
    specs = [pl.BlockSpec(memory_space=pltpu.VMEM)] * size
    aliases = {}
    if whole is not None:
        aliases = {len(args): 0}
        args.append(whole)
        specs.append(pl.BlockSpec(memory_space=pl.ANY))
    return pl.pallas_call(
        kernel,
        name="unpack",
        compiler_params=pltpu.CompilerParams(vmem_limit_bytes=GRANT),
        in_specs=specs,
        out_specs=pl.BlockSpec(memory_space=pl.ANY),
        out_shape=jax.ShapeDtypeStruct(shape, jnp.float32),
        scratch_shapes=[
            pltpu.VMEM((lanes, amount, angles, size, LANES), jnp.float32),
            pltpu.SemaphoreType.DMA((lanes,)),
        ],
        input_output_aliases=aliases,
    )(*args)


def slabs_of(chunks):
    return [lax.axis_index("hel")] if chunks == lax.axis_size("hel") else list(range(chunks))


def gather(arrays, start, stop):
    size = len(arrays)
    shape = (size, stop - start, *arrays[0].shape[1:])

    def kernel(*refs):
        ins, out, sems = refs[:size], refs[size], refs[size + 1]
        copies = [
            pltpu.make_async_copy(ins[d].at[pl.ds(start, stop - start)], out.at[d], sems.at[d])
            for d in range(size)
        ]
        for copy in copies:
            copy.start()
        for copy in copies:
            copy.wait()

    return pl.pallas_call(
        kernel,
        name="gather",
        compiler_params=pltpu.CompilerParams(vmem_limit_bytes=GRANT),
        in_specs=[pl.BlockSpec(memory_space=pl.ANY)] * size,
        out_specs=pl.BlockSpec(memory_space=pltpu.VMEM),
        out_shape=jax.ShapeDtypeStruct(shape, jnp.float32),
        scratch_shapes=[pltpu.SemaphoreType.DMA((size,))],
    )(*arrays)


def spread_potential(mine, chunks):
    groups = lax.axis_size("hel")
    if chunks != groups:
        return [mine[:, c] for c in range(chunks)]
    known = jnp.stack(swap([mine[:, 0]] * groups, "hel", range(1, groups)))
    group = lax.axis_index("hel")
    return [lax.dynamic_index_in_dim(known, jnp.bitwise_xor(group, c), keepdims=False) for c in range(chunks)]


def overlaps(spans, start, stop):
    for s, (low, high) in enumerate(spans):
        first, last = max(low, start), min(high, stop)
        if first < last:
            yield s, first - low, first - start, last - first


def edges(segments, spans):
    size = len(segments[0])
    _, angles, width = segments[0][0].shape
    count = spans[-1][1]
    jobs = [
        (side, *part)
        for side, start in enumerate((0, count - OUTER))
        for part in overlaps(spans, start, start + OUTER)
    ]

    def kernel(*refs):
        ins, targets, sems = refs[: size * len(spans)], refs[-3:-1], refs[-1]
        copies = []
        for d in range(size):
            for side, s, source, target, amount in jobs:
                copies.append(
                    pltpu.make_async_copy(
                        ins[s * size + d].at[pl.ds(source, amount)],
                        targets[side].at[d, pl.ds(target, amount)],
                        sems.at[len(copies)],
                    )
                )
                copies[-1].start()
        for copy in copies:
            copy.wait()

    shape = jax.ShapeDtypeStruct((size, OUTER, angles, width), jnp.float32)
    return pl.pallas_call(
        kernel,
        name="edges",
        compiler_params=pltpu.CompilerParams(vmem_limit_bytes=GRANT),
        in_specs=[pl.BlockSpec(memory_space=pl.ANY)] * (size * len(spans)),
        out_specs=[pl.BlockSpec(memory_space=pltpu.VMEM)] * 2,
        out_shape=[shape] * 2,
        scratch_shapes=[pltpu.SemaphoreType.DMA((len(jobs) * size,))],
    )(*[piece for segment in segments for piece in segment])


def halves(values):
    high = values.astype(jnp.bfloat16)
    return high, (values - high.astype(jnp.float32)).astype(jnp.bfloat16)


def window(segments, spans, result_spans, potential, below, above, mats, mats_below, mats_above, kinetic, radial, weights):
    size = len(segments[0])
    _, angles, width = segments[0][0].shape
    count = spans[-1][1]
    full = size * angles
    total = count + 2 * OUTER
    n_in, n_out = size * len(spans), size * len(result_spans)

    def kernel(*refs):
        weight_ref, kin_ref, rad_ref = refs[:3]
        ins = refs[3 : 3 + n_in]
        pot_ref, below_ref, above_ref, mat_ref, mat_below_ref, mat_above_ref = refs[3 + n_in : 9 + n_in]
        outs = refs[9 + n_in : 9 + n_in + n_out]
        one, two, mat, pot, kin, sems = refs[9 + n_in + n_out :]
        copies = []

        def fetch(source, target):
            copy = pltpu.make_async_copy(source, target, sems.at[len(copies)])
            copy.start()
            copies.append(copy)

        def spot(d):
            return pl.ds(pl.multiple_of(place(d) * angles, angles), angles)

        for d in range(size):
            for s, (start, stop) in enumerate(spans):
                fetch(ins[s * size + d].at[pl.ds(0, stop - start)], one.at[pl.ds(OUTER + start, stop - start), spot(d), :])
            fetch(pot_ref.at[d], pot.at[spot(d), :])
            fetch(below_ref.at[d], one.at[pl.ds(0, OUTER), spot(d), :])
            fetch(above_ref.at[d], one.at[pl.ds(OUTER + count, OUTER), spot(d), :])
        fetch(mat_below_ref, mat.at[pl.ds(0, OUTER)])
        fetch(mat_ref, mat.at[pl.ds(OUTER, count)])
        fetch(mat_above_ref, mat.at[pl.ds(OUTER + count, OUTER)])
        kin_high, kin_low = halves(kin_ref[...])
        kin[0], kin[1] = kin_high, kin_low
        for copy in copies:
            copy.wait()

        def dot(a, b):
            return jnp.dot(a, b, preferred_element_type=jnp.float32)

        def times_kinetic(field):
            high, low = halves(field)
            return dot(high, kin[0]) + dot(low, kin[0]) + dot(high, kin[1])

        def step(source, target, turn):
            first = turn + 1
            amount = total - 2 * first

            def rows(m, group):
                fields = []
                for p in range(group):
                    at = m + p - turn
                    fields.append(
                        source[at] + weight_ref[m + p + 1] * source[at + 1] + weight_ref[m + p] * source[at - 1]
                    )
                field = jnp.concatenate(fields, axis=0)
                spread = jnp.concatenate([pot[...]] * group, axis=0)
                once = times_kinetic(field) + spread * field
                mixed = 0.3 * field - 0.2 * once
                passed = 0.7 * field + times_kinetic(mixed) + spread * mixed
                for p in range(group):
                    part = passed[p * full : (p + 1) * full]
                    high, low = halves(part)
                    rows = [jnp.concatenate([piece, piece], axis=1) for piece in halves(mat[m + p])]
                    both = dot(jnp.concatenate(rows, axis=0), jnp.concatenate([high, low], axis=0))
                    target[m + p - first] = part + rad_ref[...] * (both[:full] + both[full:])

            def body(index, carry):
                rows(first + index * GROUP, GROUP)
                return carry

            lax.fori_loop(0, amount // GROUP, body, 0)
            if amount % GROUP:
                rows(first + amount // GROUP * GROUP, amount % GROUP)

        buffers = [one, two]
        for turn in range(OUTER):
            step(buffers[turn % 2], buffers[(turn + 1) % 2], turn)
        result = buffers[OUTER % 2]
        stores = []
        for d in range(size):
            for s, (start, stop) in enumerate(result_spans):
                copy = pltpu.make_async_copy(
                    result.at[pl.ds(start, stop - start), spot(d), :], outs[s * size + d], sems.at[len(stores)]
                )
                copy.start()
                stores.append(copy)
        for copy in stores:
            copy.wait()

    anywhere = pl.BlockSpec(memory_space=pl.ANY)
    results = pl.pallas_call(
        kernel,
        name="window",
        compiler_params=pltpu.CompilerParams(vmem_limit_bytes=GRANT),
        in_specs=[
            pl.BlockSpec(memory_space=pltpu.SMEM),
            pl.BlockSpec(memory_space=pltpu.VMEM),
            pl.BlockSpec(memory_space=pltpu.VMEM),
        ]
        + [anywhere] * (n_in + 6),
        out_specs=[anywhere] * n_out,
        out_shape=[
            jax.ShapeDtypeStruct((stop - start, angles, width), jnp.float32)
            for start, stop in result_spans
            for _ in range(size)
        ],
        scratch_shapes=[
            pltpu.VMEM((total, full, width), jnp.float32),
            pltpu.VMEM((total, full, width), jnp.float32),
            pltpu.VMEM((total, full, full), jnp.float32),
            pltpu.VMEM((full, width), jnp.float32),
            pltpu.VMEM((2, width, width), jnp.bfloat16),
            pltpu.SemaphoreType.DMA((max(n_in, n_out) + 3 * size + 3,)),
        ],
    )(
        weights,
        kinetic,
        radial,
        *[piece for segment in segments for piece in segment],
        potential,
        below,
        above,
        mats,
        mats_below,
        mats_above,
    )
    return [results[s * size : (s + 1) * size] for s in range(len(result_spans))]


def along_hel(array, step):
    size = lax.axis_size("hel")
    return lax.ppermute(array, "hel", [(i, i + step) for i in range(size) if 0 <= i + step < size])


def body(
    wavepacket,
    potential,
    kinetic,
    ang_basis,
    rot_energy,
    radial_weight,
    distance_weight,
    truncation,
    coupling,
):
    count, _, cells, _ = wavepacket.shape
    size = lax.axis_size("ang")
    chunks = cells // size
    ranks = sorted(range(1, size), key=lambda d: -(d // 2))
    quarter = max(count // 4, 1)
    spans = [[(0, count)] for _ in range(chunks)]
    spans[0] = [(0, quarter), (quarter, count)]
    result_spans = [[(0, count)] for _ in range(chunks)]
    tail = max(count // 8, 1)
    result_spans[-1] = [(0, count - tail), (count - tail, count)]

    received = []
    for c in range(chunks):
        segments = []
        for s, span in enumerate(spans[c]):
            sent = pack(wavepacket, c, span, potential if (c, s) == (0, 1) else None)
            segments.append(swap(sent, "ang", ranks))
        received.append(segments)
    slabs = len(slabs_of(chunks))
    potentials = spread_potential(gather(received[0][1], count - quarter, count - quarter + slabs), chunks)

    orders = jnp.arange(ang_basis.shape[1], dtype=jnp.int32)
    mask = (orders[None, :] < truncation[:, None]).astype(jnp.float32)
    factor = mask * rot_energy[None, :]
    mats = jnp.einsum(
        "kji,kjm->kim", ang_basis * factor[:, :, None], ang_basis, precision=lax.Precision.HIGHEST
    )
    mats_below = along_hel(mats[-OUTER:], 1)
    mats_above = along_hel(mats[:OUTER], -1)

    first = lax.axis_index("hel") * count
    ends = jnp.concatenate([jnp.zeros((OUTER + 1,)), coupling[:-1], jnp.zeros((OUTER + 1,))])
    near = lax.dynamic_slice_in_dim(ends, first, count + 2 * OUTER + 1)
    halos = {}
    done = {}

    def exchange(c):
        segments = received[c]
        if c >= 2:
            segments, _ = lax.optimization_barrier((segments, done[c - 2][0][0]))
        lows, highs = edges(segments, spans[c])
        halos[c] = segments, along_hel(highs, 1), along_hel(lows, -1), lows

    exchange(0)
    backs = []
    for c in range(chunks):
        weights = near * lax.dynamic_index_in_dim(
            distance_weight, c * size + lax.axis_index("ang"), keepdims=False
        )
        segments, below, above, _ = halos[c]
        if c + 1 < chunks:
            exchange(c + 1)
            weights, _ = lax.optimization_barrier((weights, halos[c + 1][3]))
        done[c] = window(
            segments,
            spans[c],
            result_spans[c],
            potentials[c],
            below,
            above,
            mats,
            mats_below,
            mats_above,
            kinetic,
            radial_weight[None],
            weights,
        )
        for s, segment in enumerate(done[c]):
            backs.append((swap(segment, "ang", ranks), c, result_spans[c][s]))
    out = None
    for back, c, span in backs:
        out = unpack(back, out, wavepacket.shape, c, span)
    return out


def solution(mesh):
    placed = (
        P("hel", "ang", None, None),
        P("ang", None, None),
        P(),
        P("hel", None, None),
        P(),
        P(),
        P(),
        P("hel"),
        P(),
    )
    whole = P("hel", "ang", None, None)
    return jax.shard_map(body, mesh=mesh, in_specs=placed, out_specs=whole, check_vma=False)
```
